32 devices in a mesh: freq: 4 (over z), tm: 2 (over core), beam: 4 (over y, x).
Axes of the slice: x: 2, y: 2, z: 4, core: 2. Of those that a mesh axis runs over, the one named last changes fastest.
Arguments:
- intensity: bfloat16 [4, 4096, 512], P('beam', 'freq', 'tm'), parts along dimension 0, may hold values from -32 to 32
- delay_tables: int32 [3, 12, 2048], replicated, may hold values from 0 to 511, as said below
- box_widths: int32 [8], replicated, may hold values from 1 to 128
Outputs:
- snr: float32 [4, 1024, 8, 512], P('beam', 'freq', None, 'tm'), parts along dimension 0
The draws below stay inside these ranges and needn't reach their ends.
There are 4 independent parts, one for each index of `beam`. The reference program is written for one: setup_inputs(seed, part) draws one part's arguments, and reference() takes and returns one part's arrays. A program takes and returns all parts, laid end to end along the dimension named above; an argument that names none is the same for every part. Nothing has to cross between parts.
Inputs may be any that keep to these rules, and one draw needn't show every extreme that they name: `delay_tables`: at merge level s (second index s - 1), with D_s = max(1, 2^(s-2)), entry [k, s-1, b D_s + d] belongs to band b and trial d; the trials (k = 0, 1) and the delay (k = 2) lie in 0 to D_(s-1) - 1; columns from (4096 / 2^s) D_s on are not read.
All inputs are finite; a program needn't handle non-finite values.
Results may differ from the reference program's by a relative error of at most 0.0003.
Values may be sent and summed in bfloat16 or wider, within the bound.
A program may use at most 64 MiB of HBM per device.

```python
import math
import jax
import jax.numpy as jnp
from jax import lax

LEVELS = 12
CHANNELS = 4096
BEAMS = 1
TIMES = 512
NWID = 8
WMAX = 128


def draw_intensity(key, part):
    noise_key = jax.random.fold_in(key, 1)
    gain_key = jax.random.fold_in(key, 2)
    stamps = jnp.arange(TIMES, dtype=jnp.float32) / max(TIMES - 1, 1)
    channel_gain = jnp.exp(jax.random.uniform(gain_key, (BEAMS, CHANNELS, 1), jnp.float32, math.log(0.5), math.log(2.0)))
    noise_field = jnp.clip(jax.random.normal(noise_key, (BEAMS, CHANNELS, TIMES), jnp.float32), -4.0, 4.0)
    time_ramp = 1.0 + 2.0 * stamps
    values = noise_field * channel_gain * time_ramp[None, None, :]
    return values.astype(jnp.bfloat16)


def draw_delay_tables(key, part):
    half_count = CHANNELS // 2
    columns = jnp.arange(half_count, dtype=jnp.int32)
    layers = []
    for merge_level in range(1, LEVELS + 1):
        depth_out = 2 ** (merge_level - 2) if merge_level >= 2 else 1
        depth_in = 2 ** (merge_level - 3) if merge_level >= 3 else 1
        used_count = (CHANNELS >> merge_level) * depth_out
        band_index = columns // depth_out
        trial_index = columns % depth_out
        fractions = jax.random.randint(jax.random.fold_in(key, merge_level), (half_count,), 8, 13, dtype=jnp.int32)
        jitters = jax.random.randint(jax.random.fold_in(key, 1000 + merge_level), (half_count,), 0, 2, dtype=jnp.int32)
        band_fraction = jnp.take(fractions, band_index)
        lower_trial = jnp.minimum(trial_index * band_fraction // 16, depth_in - 1)
        upper_trial = jnp.minimum(trial_index - lower_trial, depth_in - 1)
        delay_steps = jnp.minimum(lower_trial + jitters, depth_in - 1)
        in_use = columns < used_count
        layers.append(jnp.stack([jnp.where(in_use, lower_trial, 0), jnp.where(in_use, upper_trial, 0), jnp.where(in_use, delay_steps, 0)]))
    return jnp.stack(layers, axis=1).astype(jnp.int32)


def draw_box_widths(key, part):
    positions = jnp.arange(NWID, dtype=jnp.int32)
    base_width = jnp.maximum(jnp.right_shift(jnp.full((NWID,), WMAX, jnp.int32), NWID - 1 - positions), 1)
    extra_width = jax.random.randint(key, (NWID,), 0, 1 << 30, dtype=jnp.int32) % base_width
    widths = jnp.minimum(base_width + extra_width, WMAX)
    return jnp.where(positions == NWID - 1, WMAX, widths).astype(jnp.int32)


def setup_inputs(seed: int = 0, part: int = 0) -> dict:
    keys = jax.random.split(jax.random.key(seed), 4)
    part_splits = jax.random.split(jax.random.fold_in(keys[3], part), 4)
    return {
        "intensity": draw_intensity(jax.random.fold_in(jax.random.fold_in(keys[3], part), 71), part),
        "delay_tables": draw_delay_tables(jax.random.fold_in(keys[3], 71), part),
        "box_widths": draw_box_widths(jax.random.fold_in(keys[3], 71), part),
    }


EPSILON = 1e-05

def trial_depth(merge_level):
    if merge_level >= 2:
        return 2 ** (merge_level - 2)
    return 1

def merge_level_step(current, delay_tables, merge_level):
    bands_in, depth_in, columns = current.shape
    depth_out = trial_depth(merge_level)
    bands_out = bands_in // 2
    entries = delay_tables[:, merge_level - 1, :bands_out * depth_out].reshape(3, bands_out, depth_out)
    lower_half = current[0::2]
    upper_half = jnp.pad(current[1::2], ((0, 0), (0, 0), (0, depth_in)))
    picked = jnp.take_along_axis(lower_half, entries[0][..., None], axis=1)
    chosen = jnp.take_along_axis(upper_half, entries[1][..., None], axis=1)
    offsets = jnp.arange(columns, dtype=jnp.int32)[None, None, :] + entries[2][..., None]
    return picked + jnp.take_along_axis(chosen, offsets, axis=2)

def single_beam(beam_data, delay_tables, box_widths):
    current = beam_data.astype(jnp.float32)[:, None, :]
    for merge_level in range(1, LEVELS + 1):
        current = merge_level_step(current, delay_tables, merge_level)
    dedispersed = current[0]
    average = lax.optimization_barrier(jnp.sum(dedispersed, axis=1)) / TIMES
    centered = dedispersed - average[:, None]
    spread = lax.optimization_barrier(jnp.sum(centered * centered, axis=1)) / TIMES
    scaled = centered * lax.rsqrt(spread + EPSILON)[:, None]
    running = jnp.cumsum(jnp.pad(scaled, ((0, 0), (1, WMAX))), axis=1)
    starts = jnp.arange(TIMES, dtype=jnp.int32)
    finish = starts[None, :] + box_widths[:, None]
    boxed = running[:, finish] - running[:, starts][:, None, :]
    return boxed * lax.rsqrt(box_widths.astype(jnp.float32))[None, :, None]

def reference(intensity, delay_tables, box_widths):
    return lax.map(lambda beam_data: single_beam(beam_data, delay_tables, box_widths), intensity)
```

```python
import jax
import jax.numpy as jnp
from jax import lax
from jax.sharding import PartitionSpec as P

LEVELS = 12
WMAX = 128


EPSILON = 1e-05

BANDS = ("freq", "tm")


def band_count():
    return lax.axis_size("freq") * lax.axis_size("tm")


def swapped(block, stride):
    count = band_count()
    route = []
    for low in range(count):
        high = low | 1 << stride
        if high != low and high < count:
            route += [(low, high), (high, low)]
    return lax.ppermute(block, BANDS, route)


def trial_depth(merge_level):
    if merge_level >= 2:
        return 2 ** (merge_level - 2)
    return 1


def shift_rows(source, delays, columns, largest):
    result = source
    for bit_index in range(max(largest, 0).bit_length()):
        step_size = 1 << bit_index
        moved = jnp.concatenate(
            [result[..., step_size:], jnp.zeros_like(result[..., :step_size])], axis=-1
        )
        flag = delays >> bit_index & 1 == 1
        result = jnp.where(flag[None, :, None], moved, result)
    return result[..., :columns]


def merge_bands(current, delay_tables, merge_level, first_band):
    beam_count, bands_in, depth_in, columns = current.shape
    depth_out = trial_depth(merge_level)
    bands_out = bands_in // 2
    entries = lax.dynamic_slice_in_dim(
        delay_tables[:, merge_level - 1, :], first_band * depth_out, bands_out * depth_out, 1
    )
    band_base = jnp.arange(bands_out * depth_out, dtype=jnp.int32) // depth_out * depth_in
    lower_flat = current[:, 0::2].reshape(beam_count, bands_out * depth_in, columns)
    upper_flat = current[:, 1::2].reshape(beam_count, bands_out * depth_in, columns)
    picked = jnp.take(lower_flat, band_base + entries[0], axis=1)
    chosen = jnp.take(upper_flat, band_base + entries[1], axis=1)
    delayed = shift_rows(chosen, entries[2], columns, depth_in - 1)
    return (picked + delayed).reshape(beam_count, bands_out, depth_out, columns)


def merge_across(current, delay_tables, merge_level, cross_step, device_pos):
    beam_count, rows_held, columns = current.shape
    depth_in = rows_held * 2**cross_step
    depth_out = trial_depth(merge_level)
    group_size = 2 ** (cross_step + 1)
    position = device_pos % group_size
    upper_side = position // (group_size // 2)
    row_offset = position % (group_size // 2) * rows_held
    band_index = device_pos // group_size
    entries = lax.dynamic_slice_in_dim(
        delay_tables[:, merge_level - 1, :], band_index * depth_out, depth_out, 1
    )
    lower_local = entries[0] - row_offset
    lower_hit = (lower_local >= 0) & (lower_local < rows_held) & (upper_side == 0)
    lower_rows = jnp.take(current, jnp.clip(lower_local, 0, rows_held - 1), axis=1)
    upper_local = entries[1] - row_offset
    upper_hit = (upper_local >= 0) & (upper_local < rows_held) & (upper_side == 1)
    upper_chosen = jnp.take(current, jnp.clip(upper_local, 0, rows_held - 1), axis=1)
    upper_rows = shift_rows(upper_chosen, entries[2], columns, depth_in - 1)
    partial_value = jnp.where(lower_hit[None, :, None], lower_rows, 0.0) + jnp.where(
        upper_hit[None, :, None], upper_rows, 0.0
    )
    for bit_index in range(cross_step + 1):
        blocks = partial_value.shape[1] // rows_held
        paired = partial_value.reshape(beam_count, blocks // 2, 2, rows_held, columns)
        chosen_bit = device_pos >> bit_index & 1
        kept_rows = lax.dynamic_index_in_dim(paired, chosen_bit, 2, keepdims=False)
        given_rows = lax.dynamic_index_in_dim(paired, 1 - chosen_bit, 2, keepdims=False)
        partial_value = (kept_rows + swapped(given_rows, bit_index)).reshape(
            beam_count, blocks // 2 * rows_held, columns
        )
    return partial_value


def body(intensity, delay_tables, box_widths):
    time_parts = lax.axis_size("tm")
    time_pos = lax.axis_index("tm")
    device_pos = lax.axis_index("freq") * time_parts + time_pos
    block_len = intensity.shape[2]
    whole_rows = lax.all_to_all(intensity, "tm", 1, 2, tiled=True)
    beam_count, channels_held, time_total = whole_rows.shape
    local_levels = channels_held.bit_length() - 1
    current = whole_rows.astype(jnp.float32)[:, :, None, :]
    for merge_level in range(1, local_levels + 1):
        current = merge_bands(
            current, delay_tables, merge_level, device_pos * (channels_held >> merge_level)
        )
    dedispersed = current[:, 0]
    for cross_step in range(LEVELS - local_levels):
        dedispersed = merge_across(
            dedispersed, delay_tables, local_levels + cross_step + 1, cross_step, device_pos
        )
    average = jnp.sum(dedispersed, axis=-1) / time_total
    deviation = dedispersed - average[..., None]
    spread = jnp.sum(deviation * deviation, axis=-1) / time_total
    inverse = lax.rsqrt(spread + EPSILON)
    scaled = deviation * inverse[..., None]
    scaled = lax.all_gather(scaled, "tm", axis=1, tiled=True)
    padded = jnp.pad(scaled, ((0, 0), (0, 0), (0, WMAX)))
    window = lax.dynamic_slice_in_dim(padded, time_pos * block_len, block_len + WMAX, 2)
    running = jnp.cumsum(jnp.pad(window, ((0, 0), (0, 0), (1, 0))), axis=-1)
    leading_sum = running[..., :block_len]
    filtered = []
    for width_index in range(box_widths.shape[0]):
        ending = lax.dynamic_slice_in_dim(running, box_widths[width_index], block_len, 2)
        filtered.append(ending - leading_sum)
    boxed = jnp.stack(filtered, axis=2)
    return boxed * lax.rsqrt(box_widths.astype(jnp.float32))[None, None, :, None]


def solution(mesh):
    in_specs = (P("beam", "freq", "tm"), P(), P())
    out_specs = P("beam", "freq", None, "tm")
    return jax.shard_map(body, mesh=mesh, in_specs=in_specs, out_specs=out_specs, check_vma=False)
```

```python
import jax
import jax.numpy as jnp
from jax import lax
from jax.sharding import PartitionSpec as P

LEVELS = 12
WMAX = 128


EPSILON = 1e-05

BANDS = ("freq", "tm")


def band_count():
    return lax.axis_size("freq") * lax.axis_size("tm")


def swapped(block, stride):
    count = band_count()
    route = []
    for low in range(count):
        high = low | 1 << stride
        if high != low and high < count:
            route += [(low, high), (high, low)]
    return lax.ppermute(block, BANDS, route)


def trial_depth(merge_level):
    if merge_level >= 2:
        return 2 ** (merge_level - 2)
    return 1


def shift_rows(source, delays, columns, largest):
    result = source
    for bit_index in range(max(largest, 0).bit_length()):
        step_size = 1 << bit_index
        moved = jnp.concatenate(
            [result[..., step_size:], jnp.zeros_like(result[..., :step_size])], axis=-1
        )
        flag = delays >> bit_index & 1 == 1
        result = jnp.where(flag[None, :, None], moved, result)
    return result[..., :columns]


def merge_bands(current, delay_tables, merge_level, first_band):
    beam_count, bands_in, depth_in, columns = current.shape
    depth_out = trial_depth(merge_level)
    bands_out = bands_in // 2
    entries = lax.dynamic_slice_in_dim(
        delay_tables[:, merge_level - 1, :], first_band * depth_out, bands_out * depth_out, 1
    )
    band_base = jnp.arange(bands_out * depth_out, dtype=jnp.int32) // depth_out * depth_in
    lower_flat = current[:, 0::2].reshape(beam_count, bands_out * depth_in, columns)
    upper_flat = current[:, 1::2].reshape(beam_count, bands_out * depth_in, columns)
    picked = jnp.take(lower_flat, band_base + entries[0], axis=1)
    chosen = jnp.take(upper_flat, band_base + entries[1], axis=1)
    delayed = shift_rows(chosen, entries[2], columns, depth_in - 1)
    return (picked + delayed).reshape(beam_count, bands_out, depth_out, columns)


def merge_across(current, delay_tables, merge_level, cross_step, device_pos):
    beam_count, rows_held, columns = current.shape
    depth_in = rows_held * 2**cross_step
    depth_out = trial_depth(merge_level)
    group_size = 2 ** (cross_step + 1)
    position = device_pos % group_size
    upper_side = position // (group_size // 2)
    row_offset = position % (group_size // 2) * rows_held
    band_index = device_pos // group_size
    entries = lax.dynamic_slice_in_dim(
        delay_tables[:, merge_level - 1, :], band_index * depth_out, depth_out, 1
    )
    lower_local = entries[0] - row_offset
    lower_hit = (lower_local >= 0) & (lower_local < rows_held) & (upper_side == 0)
    lower_rows = jnp.take(current, jnp.clip(lower_local, 0, rows_held - 1), axis=1)
    upper_local = entries[1] - row_offset
    upper_hit = (upper_local >= 0) & (upper_local < rows_held) & (upper_side == 1)
    upper_chosen = jnp.take(current, jnp.clip(upper_local, 0, rows_held - 1), axis=1)
    upper_rows = shift_rows(upper_chosen, entries[2], columns, depth_in - 1)
    partial_value = jnp.where(lower_hit[None, :, None], lower_rows, 0.0) + jnp.where(
        upper_hit[None, :, None], upper_rows, 0.0
    )
    for bit_index in range(cross_step + 1):
        blocks = partial_value.shape[1] // rows_held
        paired = partial_value.reshape(beam_count, blocks // 2, 2, rows_held, columns)
        chosen_bit = device_pos >> bit_index & 1
        kept_rows = lax.dynamic_index_in_dim(paired, chosen_bit, 2, keepdims=False)
        given_rows = lax.dynamic_index_in_dim(paired, 1 - chosen_bit, 2, keepdims=False)
        partial_value = (kept_rows + swapped(given_rows, bit_index)).reshape(
            beam_count, blocks // 2 * rows_held, columns
        )
    return partial_value


def own_trials(current, delay_tables, device_pos):
    beam_count, bands_in, depth_in, columns = current.shape
    rows = trial_depth(LEVELS) // band_count()
    entries = lax.dynamic_slice_in_dim(delay_tables[:, LEVELS - 1, :], device_pos * rows, rows, 1)
    picked = jnp.take(current[:, 0], entries[0], axis=1)
    chosen = jnp.take(current[:, 1], entries[1], axis=1)
    delayed = shift_rows(chosen, entries[2], columns, depth_in - 1)
    return picked + delayed


def body(intensity, delay_tables, box_widths):
    time_parts = lax.axis_size("tm")
    time_pos = lax.axis_index("tm")
    device_pos = lax.axis_index("freq") * time_parts + time_pos
    block_len = intensity.shape[2]
    whole_rows = lax.all_to_all(intensity, "tm", 1, 2, tiled=True)
    beam_count, channels_held, time_total = whole_rows.shape
    local_levels = channels_held.bit_length() - 1
    current = whole_rows.astype(jnp.float32)[:, :, None, :]
    for merge_level in range(1, local_levels + 1):
        current = merge_bands(
            current, delay_tables, merge_level, device_pos * (channels_held >> merge_level)
        )
    merged_levels = local_levels
    if merged_levels < LEVELS:
        current = lax.all_gather(current, BANDS, axis=1, tiled=True)
        for merge_level in range(merged_levels + 1, LEVELS):
            current = merge_bands(current, delay_tables, merge_level, 0)
        dedispersed = own_trials(current, delay_tables, device_pos)
    else:
        dedispersed = current[:, 0]
    average = jnp.sum(dedispersed, axis=-1) / time_total
    deviation = dedispersed - average[..., None]
    spread = jnp.sum(deviation * deviation, axis=-1) / time_total
    inverse = lax.rsqrt(spread + EPSILON)
    scaled = deviation * inverse[..., None]
    scaled = lax.all_gather(scaled, "tm", axis=1, tiled=True)
    padded = jnp.pad(scaled, ((0, 0), (0, 0), (0, WMAX)))
    window = lax.dynamic_slice_in_dim(padded, time_pos * block_len, block_len + WMAX, 2)
    running = jnp.cumsum(jnp.pad(window, ((0, 0), (0, 0), (1, 0))), axis=-1)
    leading_sum = running[..., :block_len]
    filtered = []
    for width_index in range(box_widths.shape[0]):
        ending = lax.dynamic_slice_in_dim(running, box_widths[width_index], block_len, 2)
        filtered.append(ending - leading_sum)
    boxed = jnp.stack(filtered, axis=2)
    return boxed * lax.rsqrt(box_widths.astype(jnp.float32))[None, None, :, None]


def solution(mesh):
    in_specs = (P("beam", "freq", "tm"), P(), P())
    out_specs = P("beam", "freq", None, "tm")
    return jax.shard_map(body, mesh=mesh, in_specs=in_specs, out_specs=out_specs, check_vma=False)
```

```python
import jax
import jax.numpy as jnp
from jax import lax
from jax.sharding import PartitionSpec as P

LEVELS = 12
WMAX = 128


EPSILON = 1e-05

BANDS = ("freq", "tm")


def band_count():
    return lax.axis_size("freq") * lax.axis_size("tm")


def swapped(block, stride):
    count = band_count()
    route = []
    for low in range(count):
        high = low | 1 << stride
        if high != low and high < count:
            route += [(low, high), (high, low)]
    return lax.ppermute(block, BANDS, route)


def trial_depth(merge_level):
    if merge_level >= 2:
        return 2 ** (merge_level - 2)
    return 1


def shift_rows(source, delays, columns, largest):
    result = source
    for bit_index in range(max(largest, 0).bit_length()):
        step_size = 1 << bit_index
        moved = jnp.concatenate(
            [result[..., step_size:], jnp.zeros_like(result[..., :step_size])], axis=-1
        )
        flag = delays >> bit_index & 1 == 1
        result = jnp.where(flag[None, :, None], moved, result)
    return result[..., :columns]


def merge_bands(current, delay_tables, merge_level, first_band):
    beam_count, bands_in, depth_in, columns = current.shape
    depth_out = trial_depth(merge_level)
    bands_out = bands_in // 2
    entries = lax.dynamic_slice_in_dim(
        delay_tables[:, merge_level - 1, :], first_band * depth_out, bands_out * depth_out, 1
    )
    band_base = jnp.arange(bands_out * depth_out, dtype=jnp.int32) // depth_out * depth_in
    lower_flat = current[:, 0::2].reshape(beam_count, bands_out * depth_in, columns)
    upper_flat = current[:, 1::2].reshape(beam_count, bands_out * depth_in, columns)
    picked = jnp.take(lower_flat, band_base + entries[0], axis=1)
    chosen = jnp.take(upper_flat, band_base + entries[1], axis=1)
    delayed = shift_rows(chosen, entries[2], columns, depth_in - 1)
    return (picked + delayed).reshape(beam_count, bands_out, depth_out, columns)


def merge_across(current, delay_tables, merge_level, cross_step, device_pos):
    beam_count, rows_held, columns = current.shape
    depth_in = rows_held * 2**cross_step
    depth_out = trial_depth(merge_level)
    group_size = 2 ** (cross_step + 1)
    position = device_pos % group_size
    upper_side = position // (group_size // 2)
    row_offset = position % (group_size // 2) * rows_held
    band_index = device_pos // group_size
    entries = lax.dynamic_slice_in_dim(
        delay_tables[:, merge_level - 1, :], band_index * depth_out, depth_out, 1
    )
    lower_local = entries[0] - row_offset
    lower_hit = (lower_local >= 0) & (lower_local < rows_held) & (upper_side == 0)
    lower_rows = jnp.take(current, jnp.clip(lower_local, 0, rows_held - 1), axis=1)
    upper_local = entries[1] - row_offset
    upper_hit = (upper_local >= 0) & (upper_local < rows_held) & (upper_side == 1)
    upper_chosen = jnp.take(current, jnp.clip(upper_local, 0, rows_held - 1), axis=1)
    upper_rows = shift_rows(upper_chosen, entries[2], columns, depth_in - 1)
    partial_value = jnp.where(lower_hit[None, :, None], lower_rows, 0.0) + jnp.where(
        upper_hit[None, :, None], upper_rows, 0.0
    )
    for bit_index in range(cross_step + 1):
        blocks = partial_value.shape[1] // rows_held
        paired = partial_value.reshape(beam_count, blocks // 2, 2, rows_held, columns)
        chosen_bit = device_pos >> bit_index & 1
        kept_rows = lax.dynamic_index_in_dim(paired, chosen_bit, 2, keepdims=False)
        given_rows = lax.dynamic_index_in_dim(paired, 1 - chosen_bit, 2, keepdims=False)
        partial_value = (kept_rows + swapped(given_rows, bit_index)).reshape(
            beam_count, blocks // 2 * rows_held, columns
        )
    return partial_value


def body(intensity, delay_tables, box_widths):
    time_parts = lax.axis_size("tm")
    time_pos = lax.axis_index("tm")
    device_pos = lax.axis_index("freq") * time_parts + time_pos
    block_len = intensity.shape[2]
    whole_rows = lax.all_to_all(intensity, "tm", 1, 2, tiled=True)
    beam_count, channels_held, time_total = whole_rows.shape
    local_levels = channels_held.bit_length() - 1
    current = whole_rows.astype(jnp.float32)[:, :, None, :]
    for merge_level in range(1, local_levels + 1):
        current = merge_bands(
            current, delay_tables, merge_level, device_pos * (channels_held >> merge_level)
        )
    dedispersed = current[:, 0]
    for cross_step in range(LEVELS - local_levels):
        dedispersed = merge_across(
            dedispersed, delay_tables, local_levels + cross_step + 1, cross_step, device_pos
        )
    average = jnp.sum(dedispersed, axis=-1) / time_total
    deviation = dedispersed - average[..., None]
    spread = jnp.sum(deviation * deviation, axis=-1) / time_total
    inverse = lax.rsqrt(spread + EPSILON)
    scaled = deviation * inverse[..., None]
    padded = jnp.pad(scaled, ((0, 0), (0, 0), (0, WMAX)))
    if time_parts == 2:
        mine = lax.dynamic_slice_in_dim(padded, time_pos * block_len, block_len + WMAX, 2)
        sent = lax.dynamic_slice_in_dim(padded, (1 - time_pos) * block_len, block_len + WMAX, 2)
        theirs = lax.ppermute(sent, "tm", [(0, 1), (1, 0)])
        first = time_pos == 0
        window = jnp.concatenate(
            [jnp.where(first, mine, theirs), jnp.where(first, theirs, mine)], axis=1
        )
    else:
        padded = lax.all_gather(padded, "tm", axis=1, tiled=True)
        window = lax.dynamic_slice_in_dim(padded, time_pos * block_len, block_len + WMAX, 2)
    running = jnp.cumsum(jnp.pad(window, ((0, 0), (0, 0), (1, 0))), axis=-1)
    leading_sum = running[..., :block_len]
    filtered = []
    for width_index in range(box_widths.shape[0]):
        ending = lax.dynamic_slice_in_dim(running, box_widths[width_index], block_len, 2)
        filtered.append(ending - leading_sum)
    boxed = jnp.stack(filtered, axis=2)
    return boxed * lax.rsqrt(box_widths.astype(jnp.float32))[None, None, :, None]


def solution(mesh):
    in_specs = (P("beam", "freq", "tm"), P(), P())
    out_specs = P("beam", "freq", None, "tm")
    return jax.shard_map(body, mesh=mesh, in_specs=in_specs, out_specs=out_specs, check_vma=False)
```

```python
import jax
import jax.numpy as jnp
from jax import lax
from jax.sharding import PartitionSpec as P

LEVELS = 12
WMAX = 128


EPSILON = 1e-05

BANDS = ("freq", "tm")


def band_count():
    return lax.axis_size("freq") * lax.axis_size("tm")


def swapped(block, stride):
    count = band_count()
    route = []
    for low in range(count):
        high = low | 1 << stride
        if high != low and high < count:
            route += [(low, high), (high, low)]
    return lax.ppermute(block, BANDS, route)


def trial_depth(merge_level):
    if merge_level >= 2:
        return 2 ** (merge_level - 2)
    return 1


def shift_rows(source, delays, columns, largest):
    result = source
    for bit_index in range(max(largest, 0).bit_length()):
        step_size = 1 << bit_index
        moved = jnp.concatenate(
            [result[..., step_size:], jnp.zeros_like(result[..., :step_size])], axis=-1
        )
        flag = delays >> bit_index & 1 == 1
        result = jnp.where(flag[None, :, None], moved, result)
    return result[..., :columns]


def merge_bands(current, delay_tables, merge_level, first_band):
    beam_count, bands_in, depth_in, columns = current.shape
    depth_out = trial_depth(merge_level)
    bands_out = bands_in // 2
    entries = lax.dynamic_slice_in_dim(
        delay_tables[:, merge_level - 1, :], first_band * depth_out, bands_out * depth_out, 1
    )
    band_base = jnp.arange(bands_out * depth_out, dtype=jnp.int32) // depth_out * depth_in
    lower_flat = current[:, 0::2].reshape(beam_count, bands_out * depth_in, columns)
    upper_flat = current[:, 1::2].reshape(beam_count, bands_out * depth_in, columns)
    picked = jnp.take(lower_flat, band_base + entries[0], axis=1)
    chosen = jnp.take(upper_flat, band_base + entries[1], axis=1)
    delayed = shift_rows(chosen, entries[2], columns, depth_in - 1)
    return (picked + delayed).reshape(beam_count, bands_out, depth_out, columns)


def merge_across(current, delay_tables, merge_level, cross_step, device_pos):
    beam_count, rows_held, columns = current.shape
    depth_in = rows_held * 2**cross_step
    depth_out = trial_depth(merge_level)
    group_size = 2 ** (cross_step + 1)
    position = device_pos % group_size
    upper_side = position // (group_size // 2)
    row_offset = position % (group_size // 2) * rows_held
    band_index = device_pos // group_size
    entries = lax.dynamic_slice_in_dim(
        delay_tables[:, merge_level - 1, :], band_index * depth_out, depth_out, 1
    )
    lower_local = entries[0] - row_offset
    lower_hit = (lower_local >= 0) & (lower_local < rows_held) & (upper_side == 0)
    lower_rows = jnp.take(current, jnp.clip(lower_local, 0, rows_held - 1), axis=1)
    upper_local = entries[1] - row_offset
    upper_hit = (upper_local >= 0) & (upper_local < rows_held) & (upper_side == 1)
    upper_chosen = jnp.take(current, jnp.clip(upper_local, 0, rows_held - 1), axis=1)
    upper_rows = shift_rows(upper_chosen, entries[2], columns, depth_in - 1)
    partial_value = jnp.where(lower_hit[None, :, None], lower_rows, 0.0) + jnp.where(
        upper_hit[None, :, None], upper_rows, 0.0
    )
    for bit_index in range(cross_step + 1):
        blocks = partial_value.shape[1] // rows_held
        paired = partial_value.reshape(beam_count, blocks // 2, 2, rows_held, columns)
        chosen_bit = device_pos >> bit_index & 1
        kept_rows = lax.dynamic_index_in_dim(paired, chosen_bit, 2, keepdims=False)
        given_rows = lax.dynamic_index_in_dim(paired, 1 - chosen_bit, 2, keepdims=False)
        partial_value = (kept_rows + swapped(given_rows, bit_index)).reshape(
            beam_count, blocks // 2 * rows_held, columns
        )
    return partial_value


def body(intensity, delay_tables, box_widths):
    time_parts = lax.axis_size("tm")
    time_pos = lax.axis_index("tm")
    device_pos = lax.axis_index("freq") * time_parts + time_pos
    block_len = intensity.shape[2]
    whole_rows = lax.all_to_all(intensity.astype(jnp.float32), "tm", 1, 2, tiled=True)
    beam_count, channels_held, time_total = whole_rows.shape
    local_levels = channels_held.bit_length() - 1
    current = whole_rows[:, :, None, :]
    for merge_level in range(1, local_levels + 1):
        current = merge_bands(
            current, delay_tables, merge_level, device_pos * (channels_held >> merge_level)
        )
    dedispersed = current[:, 0]
    for cross_step in range(LEVELS - local_levels):
        dedispersed = merge_across(
            dedispersed, delay_tables, local_levels + cross_step + 1, cross_step, device_pos
        )
    average = jnp.sum(dedispersed, axis=-1) / time_total
    deviation = dedispersed - average[..., None]
    spread = jnp.sum(deviation * deviation, axis=-1) / time_total
    inverse = lax.rsqrt(spread + EPSILON)
    scaled = deviation * inverse[..., None]
    padded = jnp.pad(scaled, ((0, 0), (0, 0), (0, WMAX)))
    if time_parts == 2:
        mine = lax.dynamic_slice_in_dim(padded, time_pos * block_len, block_len + WMAX, 2)
        sent = lax.dynamic_slice_in_dim(padded, (1 - time_pos) * block_len, block_len + WMAX, 2)
        theirs = lax.ppermute(sent, "tm", [(0, 1), (1, 0)])
        first = time_pos == 0
        window = jnp.concatenate(
            [jnp.where(first, mine, theirs), jnp.where(first, theirs, mine)], axis=1
        )
    else:
        padded = lax.all_gather(padded, "tm", axis=1, tiled=True)
        window = lax.dynamic_slice_in_dim(padded, time_pos * block_len, block_len + WMAX, 2)
    running = jnp.cumsum(jnp.pad(window, ((0, 0), (0, 0), (1, 0))), axis=-1)
    leading_sum = running[..., :block_len]
    filtered = []
    for width_index in range(box_widths.shape[0]):
        ending = lax.dynamic_slice_in_dim(running, box_widths[width_index], block_len, 2)
        filtered.append(ending - leading_sum)
    boxed = jnp.stack(filtered, axis=2)
    return boxed * lax.rsqrt(box_widths.astype(jnp.float32))[None, None, :, None]


def solution(mesh):
    in_specs = (P("beam", "freq", "tm"), P(), P())
    out_specs = P("beam", "freq", None, "tm")
    return jax.shard_map(body, mesh=mesh, in_specs=in_specs, out_specs=out_specs, check_vma=False)
```

```python
import jax
import jax.numpy as jnp
from jax import lax
from jax.sharding import PartitionSpec as P

LEVELS = 12
WMAX = 128


EPSILON = 1e-05

BANDS = ("freq", "tm")


def band_count():
    return lax.axis_size("freq") * lax.axis_size("tm")


def swapped(block, stride):
    count = band_count()
    route = []
    for low in range(count):
        high = low | 1 << stride
        if high != low and high < count:
            route += [(low, high), (high, low)]
    return lax.ppermute(block, BANDS, route)


def trial_depth(merge_level):
    if merge_level >= 2:
        return 2 ** (merge_level - 2)
    return 1


def shift_rows(source, delays, columns, largest):
    result = source
    for bit_index in range(max(largest, 0).bit_length()):
        step_size = 1 << bit_index
        moved = jnp.concatenate(
            [result[..., step_size:], jnp.zeros_like(result[..., :step_size])], axis=-1
        )
        flag = delays >> bit_index & 1 == 1
        result = jnp.where(flag[None, :, None], moved, result)
    return result[..., :columns]


def merge_bands(current, delay_tables, merge_level, first_band):
    beam_count, bands_in, depth_in, columns = current.shape
    depth_out = trial_depth(merge_level)
    bands_out = bands_in // 2
    entries = lax.dynamic_slice_in_dim(
        delay_tables[:, merge_level - 1, :], first_band * depth_out, bands_out * depth_out, 1
    )
    band_base = jnp.arange(bands_out * depth_out, dtype=jnp.int32) // depth_out * depth_in
    lower_flat = current[:, 0::2].reshape(beam_count, bands_out * depth_in, columns)
    upper_flat = current[:, 1::2].reshape(beam_count, bands_out * depth_in, columns)
    picked = jnp.take(lower_flat, band_base + entries[0], axis=1)
    chosen = jnp.take(upper_flat, band_base + entries[1], axis=1)
    delayed = shift_rows(chosen, entries[2], columns, depth_in - 1)
    return (picked + delayed).reshape(beam_count, bands_out, depth_out, columns)


def merge_across(current, delay_tables, merge_level, cross_step, device_pos):
    beam_count, rows_held, columns = current.shape
    depth_in = rows_held * 2**cross_step
    depth_out = trial_depth(merge_level)
    group_size = 2 ** (cross_step + 1)
    position = device_pos % group_size
    upper_side = position // (group_size // 2)
    row_offset = position % (group_size // 2) * rows_held
    band_index = device_pos // group_size
    entries = lax.dynamic_slice_in_dim(
        delay_tables[:, merge_level - 1, :], band_index * depth_out, depth_out, 1
    )
    lower_local = entries[0] - row_offset
    lower_hit = (lower_local >= 0) & (lower_local < rows_held) & (upper_side == 0)
    lower_rows = jnp.take(current, jnp.clip(lower_local, 0, rows_held - 1), axis=1)
    upper_local = entries[1] - row_offset
    upper_hit = (upper_local >= 0) & (upper_local < rows_held) & (upper_side == 1)
    upper_chosen = jnp.take(current, jnp.clip(upper_local, 0, rows_held - 1), axis=1)
    upper_rows = shift_rows(upper_chosen, entries[2], columns, depth_in - 1)
    partial_value = jnp.where(lower_hit[None, :, None], lower_rows, 0.0) + jnp.where(
        upper_hit[None, :, None], upper_rows, 0.0
    )
    remaining = list(range(cross_step + 1))
    for bit_index in [0] + list(range(cross_step, 0, -1)):
        place = remaining.index(bit_index)
        remaining.remove(bit_index)
        below = 2**place * rows_held
        paired = partial_value.reshape(beam_count, -1, 2, below, columns)
        chosen_bit = device_pos >> bit_index & 1
        kept_rows = lax.dynamic_index_in_dim(paired, chosen_bit, 2, keepdims=False)
        given_rows = lax.dynamic_index_in_dim(paired, 1 - chosen_bit, 2, keepdims=False)
        partial_value = (kept_rows + swapped(given_rows, bit_index)).reshape(
            beam_count, -1, columns
        )
    return partial_value


def body(intensity, delay_tables, box_widths):
    time_parts = lax.axis_size("tm")
    time_pos = lax.axis_index("tm")
    device_pos = lax.axis_index("freq") * time_parts + time_pos
    block_len = intensity.shape[2]
    whole_rows = lax.all_to_all(intensity.astype(jnp.float32), "tm", 1, 2, tiled=True)
    beam_count, channels_held, time_total = whole_rows.shape
    local_levels = channels_held.bit_length() - 1
    current = whole_rows[:, :, None, :]
    for merge_level in range(1, local_levels + 1):
        current = merge_bands(
            current, delay_tables, merge_level, device_pos * (channels_held >> merge_level)
        )
    dedispersed = current[:, 0]
    for cross_step in range(LEVELS - local_levels):
        dedispersed = merge_across(
            dedispersed, delay_tables, local_levels + cross_step + 1, cross_step, device_pos
        )
    average = jnp.sum(dedispersed, axis=-1) / time_total
    deviation = dedispersed - average[..., None]
    spread = jnp.sum(deviation * deviation, axis=-1) / time_total
    inverse = lax.rsqrt(spread + EPSILON)
    scaled = deviation * inverse[..., None]
    padded = jnp.pad(scaled, ((0, 0), (0, 0), (0, WMAX)))
    if time_parts == 2:
        mine = lax.dynamic_slice_in_dim(padded, time_pos * block_len, block_len + WMAX, 2)
        sent = lax.dynamic_slice_in_dim(padded, (1 - time_pos) * block_len, block_len + WMAX, 2)
        theirs = lax.ppermute(sent, "tm", [(0, 1), (1, 0)])
        first = time_pos == 0
        window = jnp.concatenate(
            [jnp.where(first, mine, theirs), jnp.where(first, theirs, mine)], axis=1
        )
    else:
        padded = lax.all_gather(padded, "tm", axis=1, tiled=True)
        window = lax.dynamic_slice_in_dim(padded, time_pos * block_len, block_len + WMAX, 2)
    running = jnp.cumsum(jnp.pad(window, ((0, 0), (0, 0), (1, 0))), axis=-1)
    leading_sum = running[..., :block_len]
    filtered = []
    for width_index in range(box_widths.shape[0]):
        ending = lax.dynamic_slice_in_dim(running, box_widths[width_index], block_len, 2)
        filtered.append(ending - leading_sum)
    boxed = jnp.stack(filtered, axis=2)
    return boxed * lax.rsqrt(box_widths.astype(jnp.float32))[None, None, :, None]


def solution(mesh):
    in_specs = (P("beam", "freq", "tm"), P(), P())
    out_specs = P("beam", "freq", None, "tm")
    return jax.shard_map(body, mesh=mesh, in_specs=in_specs, out_specs=out_specs, check_vma=False)
```

```python
import jax
import jax.numpy as jnp
from jax import lax
from jax.sharding import PartitionSpec as P

LEVELS = 12
WMAX = 128


EPSILON = 1e-05

BANDS = ("freq", "tm")


def band_count():
    return lax.axis_size("freq") * lax.axis_size("tm")


def swapped(block, stride):
    count = band_count()
    route = []
    for low in range(count):
        high = low | 1 << stride
        if high != low and high < count:
            route += [(low, high), (high, low)]
    return lax.ppermute(block, BANDS, route)


def trial_depth(merge_level):
    if merge_level >= 2:
        return 2 ** (merge_level - 2)
    return 1


def shift_rows(source, delays, columns, largest):
    result = source
    for bit_index in range(max(largest, 0).bit_length()):
        step_size = 1 << bit_index
        moved = jnp.concatenate(
            [result[..., step_size:], jnp.zeros_like(result[..., :step_size])], axis=-1
        )
        flag = delays >> bit_index & 1 == 1
        result = jnp.where(flag[None, :, None], moved, result)
    return result[..., :columns]


def merge_bands(current, delay_tables, merge_level, first_band):
    beam_count, bands_in, depth_in, columns = current.shape
    depth_out = trial_depth(merge_level)
    bands_out = bands_in // 2
    entries = lax.dynamic_slice_in_dim(
        delay_tables[:, merge_level - 1, :], first_band * depth_out, bands_out * depth_out, 1
    )
    band_base = jnp.arange(bands_out * depth_out, dtype=jnp.int32) // depth_out * depth_in
    lower_flat = current[:, 0::2].reshape(beam_count, bands_out * depth_in, columns)
    upper_flat = current[:, 1::2].reshape(beam_count, bands_out * depth_in, columns)
    picked = jnp.take(lower_flat, band_base + entries[0], axis=1)
    chosen = jnp.take(upper_flat, band_base + entries[1], axis=1)
    delayed = shift_rows(chosen, entries[2], columns, depth_in - 1)
    return (picked + delayed).reshape(beam_count, bands_out, depth_out, columns)


def merge_across(current, delay_tables, merge_level, cross_step, device_pos):
    beam_count, rows_held, columns = current.shape
    depth_in = rows_held * 2**cross_step
    depth_out = trial_depth(merge_level)
    group_size = 2 ** (cross_step + 1)
    position = device_pos % group_size
    upper_side = position // (group_size // 2)
    row_offset = position % (group_size // 2) * rows_held
    band_index = device_pos // group_size
    entries = lax.dynamic_slice_in_dim(
        delay_tables[:, merge_level - 1, :], band_index * depth_out, depth_out, 1
    )
    lower_local = entries[0] - row_offset
    lower_hit = (lower_local >= 0) & (lower_local < rows_held) & (upper_side == 0)
    lower_rows = jnp.take(current, jnp.clip(lower_local, 0, rows_held - 1), axis=1)
    upper_local = entries[1] - row_offset
    upper_hit = (upper_local >= 0) & (upper_local < rows_held) & (upper_side == 1)
    upper_chosen = jnp.take(current, jnp.clip(upper_local, 0, rows_held - 1), axis=1)
    upper_rows = shift_rows(upper_chosen, entries[2], columns, depth_in - 1)
    partial_value = jnp.where(lower_hit[None, :, None], lower_rows, 0.0) + jnp.where(
        upper_hit[None, :, None], upper_rows, 0.0
    )
    blocks = partial_value.reshape(beam_count, group_size, rows_held, columns)
    total = lax.dynamic_index_in_dim(blocks, position, 1, keepdims=False)
    for offset in range(1, group_size):
        sent = lax.dynamic_index_in_dim(blocks, position ^ offset, 1, keepdims=False)
        route = [(low, low ^ offset) for low in range(band_count())]
        total = total + lax.ppermute(sent, BANDS, route)
    partial_value = total
    return partial_value


def body(intensity, delay_tables, box_widths):
    time_parts = lax.axis_size("tm")
    time_pos = lax.axis_index("tm")
    device_pos = lax.axis_index("freq") * time_parts + time_pos
    block_len = intensity.shape[2]
    whole_rows = lax.all_to_all(intensity.astype(jnp.float32), "tm", 1, 2, tiled=True)
    beam_count, channels_held, time_total = whole_rows.shape
    local_levels = channels_held.bit_length() - 1
    current = whole_rows[:, :, None, :]
    for merge_level in range(1, local_levels + 1):
        current = merge_bands(
            current, delay_tables, merge_level, device_pos * (channels_held >> merge_level)
        )
    dedispersed = current[:, 0]
    for cross_step in range(LEVELS - local_levels):
        dedispersed = merge_across(
            dedispersed, delay_tables, local_levels + cross_step + 1, cross_step, device_pos
        )
    average = jnp.sum(dedispersed, axis=-1) / time_total
    deviation = dedispersed - average[..., None]
    spread = jnp.sum(deviation * deviation, axis=-1) / time_total
    inverse = lax.rsqrt(spread + EPSILON)
    scaled = deviation * inverse[..., None]
    padded = jnp.pad(scaled, ((0, 0), (0, 0), (0, WMAX)))
    if time_parts == 2:
        mine = lax.dynamic_slice_in_dim(padded, time_pos * block_len, block_len + WMAX, 2)
        sent = lax.dynamic_slice_in_dim(padded, (1 - time_pos) * block_len, block_len + WMAX, 2)
        theirs = lax.ppermute(sent, "tm", [(0, 1), (1, 0)])
        first = time_pos == 0
        window = jnp.concatenate(
            [jnp.where(first, mine, theirs), jnp.where(first, theirs, mine)], axis=1
        )
    else:
        padded = lax.all_gather(padded, "tm", axis=1, tiled=True)
        window = lax.dynamic_slice_in_dim(padded, time_pos * block_len, block_len + WMAX, 2)
    running = jnp.cumsum(jnp.pad(window, ((0, 0), (0, 0), (1, 0))), axis=-1)
    leading_sum = running[..., :block_len]
    filtered = []
    for width_index in range(box_widths.shape[0]):
        ending = lax.dynamic_slice_in_dim(running, box_widths[width_index], block_len, 2)
        filtered.append(ending - leading_sum)
    boxed = jnp.stack(filtered, axis=2)
    return boxed * lax.rsqrt(box_widths.astype(jnp.float32))[None, None, :, None]


def solution(mesh):
    in_specs = (P("beam", "freq", "tm"), P(), P())
    out_specs = P("beam", "freq", None, "tm")
    return jax.shard_map(body, mesh=mesh, in_specs=in_specs, out_specs=out_specs, check_vma=False)
```
